512 devices in a mesh: pair: 256 (over z, y, x), aux: 2 (over core).
Axes of the slice: x: 4, y: 8, z: 8, core: 2. Of those that a mesh axis runs over, the one named last changes fastest.
Arguments:
- amplitudes: bfloat16 [256, 256, 256], P('pair'), may hold values from -6 to 6
- ranks: int32 [256], P('pair'), may hold values from 64 to 256
- neighbours: int32 [256, 16], P('pair', 'aux'), may hold values from 0 to 255, as said below
- intersections: bfloat16 [256, 16, 256, 256], P('pair', 'aux'), may hold values from -0.375 to 0.375
- couplings: float32 [256, 16], P('pair', 'aux'), may hold values from -1 to 1
- energies: float32 [256, 256], P('pair'), may hold values from 0.5 to 4
- factors: bfloat16 [256, 2, 5120, 256], P('pair', None, 'aux'), may hold values from -1.75 to 1.75
Outputs:
- residual: float32 [256, 256, 256], P('pair', 'aux')
- updated: float32 [256, 256, 256], P('pair', 'aux')
The draws below stay inside these ranges and needn't reach their ends.
Inputs may be any that keep to these rules, and one draw needn't show every extreme that they name: `neighbours`: the 16 coupled pairs of pair p are distinct and lie among the pairs p - 8 to p + 8, counted modulo 256.
All inputs are finite; a program needn't handle non-finite values.
Results may differ from the reference program's by a relative error of at most 0.0022.
Values may be sent and summed in bfloat16 or wider, within the bound.
A program may use at most 64 MiB of HBM per device.

```python
import math
import jax
import jax.numpy as jnp
from jax import lax

R = 256
NAUX = 5120
NBR = 16
WIN = 8
PAIRS = 256


def draw_neighbours(key, part):
    keys = jax.random.split(key, PAIRS)
    offsets = jnp.arange(2 * WIN + 1, dtype=jnp.int32) - WIN

    def one_row(row_key):
        return jax.random.permutation(row_key, offsets)[:NBR]
    picked = jax.vmap(one_row)(keys)
    anchor = jnp.arange(PAIRS, dtype=jnp.int32)
    return ((anchor[:, None] + picked) % PAIRS).astype(jnp.int32)


def touch_ends(array, rng, least, high):
    spot = [jax.random.randint(jax.random.fold_in(rng, axis), (), 0, length) for axis, length in enumerate(array.shape)]
    longest = array.shape.index(max(array.shape))
    next_to = spot[:longest] + [(spot[longest] + 1) % array.shape[longest]] + spot[longest + 1:]
    return array.at[tuple(spot)].set(least).at[tuple(next_to)].set(high)


def steps_of(own_key, dims, shards, smallest, high):
    level, own = 1.0, jax.random.fold_in(own_key, 6)
    for axis_at, blocks in shards:
        heights = jnp.exp(jax.random.uniform(jax.random.fold_in(own, axis_at), (blocks,), jnp.float32, smallest / len(shards), high / len(shards)))
        level = level * jnp.repeat(heights, dims[axis_at] // blocks).reshape([-1 if axis == axis_at else 1 for axis in range(len(dims))])
    return level


def gaussian(key, dims, spread, most, cuts=(), held_as=jnp.bfloat16):
    array = spread * jax.random.normal(key, dims, jnp.float32)
    if cuts:
        array = array * steps_of(key, dims, cuts, -0.22, 0.18)
    return jnp.clip(array, -most, most).astype(held_as)


def setup_inputs(seed: int = 0) -> dict:
    seeds = jax.random.split(jax.random.key(seed), 8)
    amplitudes = gaussian(seeds[0], (PAIRS, R, R), 1.0, 6.0, ((0, 256),))
    ranks = touch_ends(jax.random.randint(seeds[1], (PAIRS,), R // 4, R + 1), jax.random.fold_in(seeds[1], 1), R // 4, R).astype(jnp.int32)
    neighbours = draw_neighbours(jax.random.fold_in(seeds[7], 71), 0)
    intersections = gaussian(seeds[3], (PAIRS, NBR, R, R), R ** -0.5, 0.375, ((0, 256), (1, 2)))
    couplings = jnp.clip(jax.random.uniform(seeds[4], (PAIRS, NBR), jnp.float32, -1.0, 1.0) * steps_of(seeds[4], (PAIRS, NBR), ((0, 256), (1, 2)), -0.4, 0.0), -1.0, 1.0)
    energies = jnp.clip(jnp.exp(math.log(4.0) - 2.0794415 * jax.random.uniform(seeds[5], (PAIRS, R), jnp.float32) ** steps_of(seeds[5], (PAIRS, R), ((0, 256),), -0.2, 0.2)), 0.5, 4.0)
    factors = gaussian(seeds[6], (PAIRS, 2, NAUX, R), (NAUX ** -0.25), 1.75, ((0, 256), (2, 2)))
    return {"amplitudes": amplitudes, "ranks": ranks, "neighbours": neighbours, "intersections": intersections, "couplings": couplings, "energies": energies, "factors": factors}


def reference(amplitudes, ranks, neighbours, intersections, couplings, energies, factors):
    positions = jnp.arange(R)
    live_rows = positions[None, :] < ranks[:, None]
    square_mask = live_rows[:, :, None] & live_rows[:, None, :]
    masked = jnp.where(square_mask, amplitudes, jnp.zeros((), amplitudes.dtype))

    def one_pair(index):
        pair_factors = factors[index]
        partial_sum = jnp.dot(pair_factors[0].T, pair_factors[1], preferred_element_type=jnp.float32)
        for column in range(NBR):
            picked = masked[neighbours[index, column]]
            intersection_now = intersections[index, column]
            half_product = jnp.dot(intersection_now, picked, preferred_element_type=jnp.float32).astype(jnp.bfloat16)
            projected = jnp.dot(half_product, intersection_now.T, preferred_element_type=jnp.float32)
            partial_sum = partial_sum + couplings[index, column] * projected
        energy_row = energies[index]
        denominator = energy_row[:, None] + energy_row[None, :]
        own_amp = masked[index].astype(jnp.float32)
        residual = jnp.where(square_mask[index], partial_sum + denominator * own_amp, jnp.zeros((), jnp.float32))
        return residual, own_amp - residual / denominator

    residual, updated = lax.map(one_pair, jnp.arange(PAIRS))
    return residual, updated
```

```python
import functools

import jax
import jax.numpy as jnp
from jax import lax
from jax.experimental import pallas as pl
from jax.experimental.pallas import tpu as pltpu
from jax.sharding import PartitionSpec as P

WIN = 8
MESH = pl.DeviceIdType.MESH


def body(
    pairs,
    amp_hbm,
    ranks_hbm,
    nbr_hbm,
    inter_hbm,
    coup_hbm,
    energy_hbm,
    fact_hbm,
    res_ref,
    upd_ref,
    tbuf,
    sbuf,
    fbuf,
    acc,
    send_half,
    recv_half,
    own_rows,
    energy,
    rank_s,
    nbr_s,
    coup_s,
    loc_sem,
    s_send,
    s_recv,
    t_send,
    t_recv,
    r_sem,
):
    width = amp_hbm.shape[1]
    half_w = width // 2
    slots = nbr_hbm.shape[1]
    p = lax.axis_index("pair")
    c = lax.axis_index("aux")
    other = 1 - c
    sibling = (p, other)
    cols = pl.ds(pl.multiple_of(c * half_w, half_w), half_w)

    def local(src, dst, k):
        return pltpu.make_async_copy(src, dst, loc_sem.at[k])

    loads = [
        local(ranks_hbm, rank_s, 0),
        local(amp_hbm.at[0, :, cols], tbuf.at[WIN], 1),
        local(amp_hbm.at[0, cols, :], own_rows, 2),
        local(nbr_hbm.at[0], nbr_s.at[c], 3),
        local(coup_hbm.at[0], coup_s.at[c], 4),
        local(energy_hbm, energy, 5),
        local(fact_hbm.at[0], fbuf, 6),
        local(inter_hbm.at[0], sbuf.at[pl.ds(c * slots, slots)], 7),
    ]
    for copy in loads:
        copy.start()

    barrier = pltpu.get_barrier_semaphore()
    pl.semaphore_signal(barrier, inc=1, device_id=sibling, device_id_type=MESH)
    for step in range(1, WIN + 1):
        for sign in (1, -1):
            peer = lax.rem(p + sign * step + pairs, pairs)
            pl.semaphore_signal(barrier, inc=1, device_id=(peer, c), device_id_type=MESH)

    loads[0].wait()
    loads[1].wait()
    rank = rank_s[0]
    row_id = lax.broadcasted_iota(jnp.int32, (width, half_w), 0)
    col_id = lax.broadcasted_iota(jnp.int32, (width, half_w), 1) + c * half_w
    tbuf[WIN] = jnp.where((row_id < rank) & (col_id < rank), tbuf[WIN].astype(jnp.float32), 0.0).astype(jnp.bfloat16)

    pl.semaphore_wait(barrier, 2 * WIN + 1)

    sends = []
    for step in range(WIN, 0, -1):
        for sign in (1, -1):
            peer = lax.rem(p + sign * step + pairs, pairs)
            place = WIN - sign * step
            sends.append(
                pltpu.make_async_remote_copy(
                    src_ref=tbuf.at[WIN],
                    dst_ref=tbuf.at[place],
                    send_sem=t_send.at[place],
                    recv_sem=t_recv.at[place],
                    device_id=(peer, c),
                    device_id_type=MESH,
                )
            )
    for copy in sends:
        copy.start()
    shares = []
    for k, (src, dst) in enumerate(
        (
            (nbr_hbm.at[0], nbr_s.at[c]),
            (coup_hbm.at[0], coup_s.at[c]),
            (inter_hbm.at[0], sbuf.at[pl.ds(c * slots, slots)]),
        )
    ):
        shares.append(
            pltpu.make_async_remote_copy(
                src_ref=src, dst_ref=dst, send_sem=s_send.at[k], recv_sem=s_recv.at[k],
                device_id=sibling, device_id_type=MESH,
            )
        )
    for copy in shares:
        copy.start()

    loads[6].wait()
    acc[...] = lax.dot_general(
        fbuf[0], fbuf[1], (((0,), (0,)), ((), ())), preferred_element_type=jnp.float32
    )
    for k in (2, 3, 4, 5, 7):
        loads[k].wait()
    for copy in shares:
        copy.wait()

    def couple(w):
        slot = jnp.int32(0)
        factor = jnp.float32(0)
        for core in range(2):
            for n in range(slots):
                hit = lax.rem(nbr_s[core, n] - p + WIN + pairs, pairs) == w
                slot = jnp.where(hit, core * slots + n, slot)
                factor = jnp.where(hit, coup_s[core, n], factor)
        near = sbuf[slot]
        half = jnp.dot(near, tbuf[w], preferred_element_type=jnp.float32).astype(jnp.bfloat16)
        near_cols = sbuf[slot, :, cols]
        projected = lax.dot_general(
            half, near_cols, (((1,), (1,)), ((), ())), preferred_element_type=jnp.float32
        )
        acc[...] += factor * projected

    couple(WIN)

    @pl.loop(0, WIN)
    def _(k):
        step = WIN - k
        for sign in (1, -1):
            place = WIN - sign * step
            pltpu.make_async_copy(tbuf.at[place], tbuf.at[place], t_recv.at[place]).wait()
            couple(place)

    theirs = pl.ds(pl.multiple_of(other * half_w, half_w), half_w)
    send_half[...] = acc[theirs, :]
    ship = pltpu.make_async_remote_copy(
        src_ref=send_half, dst_ref=recv_half, send_sem=r_sem.at[0], recv_sem=r_sem.at[1],
        device_id=sibling, device_id_type=MESH,
    )
    ship.start()
    rows = lax.broadcasted_iota(jnp.int32, (half_w, width), 0) + c * half_w
    columns = lax.broadcasted_iota(jnp.int32, (half_w, width), 1)
    live = (rows < rank) & (columns < rank)
    by_row = jnp.transpose(jnp.broadcast_to(energy[:, cols], (half_w, half_w)))
    denominator = jnp.concatenate([by_row, by_row], axis=1) + energy[...]
    own = jnp.where(live, own_rows[...].astype(jnp.float32), 0.0)
    for copy in sends:
        copy.wait_send()
    ship.wait()
    summed = acc[cols, :] + recv_half[...]
    residual = jnp.where(live, summed + denominator * own, 0.0)
    res_ref[0] = residual
    upd_ref[0] = own - residual / denominator


def shards(amplitudes, ranks, neighbours, intersections, couplings, energies, factors):
    pairs = lax.axis_size("pair")
    width = amplitudes.shape[1]
    half_w = width // 2
    slots = neighbours.shape[1]
    span = factors.shape[2]
    out = jax.ShapeDtypeStruct((1, half_w, width), jnp.float32)
    any_spec = pl.BlockSpec(memory_space=pl.ANY)
    vmem = pl.BlockSpec(memory_space=pltpu.VMEM)
    dma = pltpu.SemaphoreType.DMA
    return pl.pallas_call(
        functools.partial(body, pairs),
        out_shape=(out, out),
        in_specs=[any_spec] * 7,
        out_specs=(vmem, vmem),
        scratch_shapes=[
            pltpu.VMEM((2 * WIN + 1, width, half_w), jnp.bfloat16),
            pltpu.VMEM((2 * slots, width, width), jnp.bfloat16),
            pltpu.VMEM((2, span, width), jnp.bfloat16),
            pltpu.VMEM((width, width), jnp.float32),
            pltpu.VMEM((half_w, width), jnp.float32),
            pltpu.VMEM((half_w, width), jnp.float32),
            pltpu.VMEM((half_w, width), jnp.bfloat16),
            pltpu.VMEM((1, width), jnp.float32),
            pltpu.SMEM((1,), jnp.int32),
            pltpu.SMEM((2, slots), jnp.int32),
            pltpu.SMEM((2, slots), jnp.float32),
            dma((8,)),
            dma((3,)),
            dma((3,)),
            dma((2 * WIN + 1,)),
            dma((2 * WIN + 1,)),
            dma((2,)),
        ],
        compiler_params=pltpu.CompilerParams(
            collective_id=0, has_side_effects=True
        ),
    )(amplitudes, ranks, neighbours, intersections, couplings, energies, factors)


def solution(mesh):
    return jax.shard_map(
        shards,
        mesh=mesh,
        in_specs=(
            P("pair", None, None),
            P("pair"),
            P("pair", "aux"),
            P("pair", "aux", None, None),
            P("pair", "aux"),
            P("pair", None),
            P("pair", None, "aux", None),
        ),
        out_specs=(P("pair", "aux", None), P("pair", "aux", None)),
        check_vma=False,
    )
```

```python
import functools

import jax
import jax.numpy as jnp
from jax import lax
from jax.experimental import pallas as pl
from jax.experimental.pallas import tpu as pltpu
from jax.sharding import PartitionSpec as P

WIN = 8
RING = 4
REACH = WIN // RING
MESH = pl.DeviceIdType.MESH


def body(
    pairs,
    amp_hbm,
    ranks_hbm,
    nbr_hbm,
    inter_hbm,
    coup_hbm,
    energy_hbm,
    fact_hbm,
    res_ref,
    upd_ref,
    tbuf,
    sbuf,
    fbuf,
    acc,
    send_half,
    recv_half,
    own_rows,
    energy,
    rank_s,
    nbr_s,
    coup_s,
    slot_s,
    factor_s,
    loc_sem,
    s_send,
    s_recv,
    t_send,
    t_recv,
    r_sem,
):
    width = amp_hbm.shape[1]
    half_w = width // 2
    slots = nbr_hbm.shape[1]
    rows_all = pairs // RING
    p = lax.axis_index("pair")
    c = lax.axis_index("aux")
    other = 1 - c
    sibling = (p, other)
    x = lax.rem(p, RING)
    row = p // RING
    cols = pl.ds(pl.multiple_of(c * half_w, half_w), half_w)

    def column(dx):
        return lax.rem(x + dx + RING, RING)

    def far_row(dy):
        return lax.rem(row + dy + rows_all, rows_all)

    def chip(dx, dy):
        return (far_row(dy) * RING + column(dx), c)

    def local(src, dst, k):
        return pltpu.make_async_copy(src, dst, loc_sem.at[k])

    own_tile = tbuf.at[REACH, x]
    loads = [
        local(ranks_hbm, rank_s, 0),
        local(amp_hbm.at[0, :, cols], own_tile, 1),
        local(nbr_hbm.at[0], nbr_s.at[c], 2),
        local(coup_hbm.at[0], coup_s.at[c], 3),
        local(fact_hbm.at[0], fbuf, 4),
        local(inter_hbm.at[0], sbuf.at[pl.ds(c * slots, slots)], 5),
        local(amp_hbm.at[0, cols, :], own_rows, 6),
        local(energy_hbm, energy, 7),
    ]
    for copy in loads:
        copy.start()

    barrier = pltpu.get_barrier_semaphore()
    row_steps = (1, -1, 2, -2)
    peers = [sibling]
    peers += [chip(0, dy) for dy in row_steps]
    peers += [chip(dx, 0) for dx in (1, 2, 3)]
    for peer in peers:
        pl.semaphore_signal(barrier, inc=1, device_id=peer, device_id_type=MESH)

    loads[0].wait()
    loads[1].wait()
    rank = rank_s[0]
    row_id = lax.broadcasted_iota(jnp.int32, (width, half_w), 0)
    col_id = lax.broadcasted_iota(jnp.int32, (width, half_w), 1) + c * half_w
    own_tile[...] = jnp.where(
        (row_id < rank) & (col_id < rank), own_tile[...].astype(jnp.float32), 0.0
    ).astype(jnp.bfloat16)

    pl.semaphore_wait(barrier, len(peers))

    def send(tile, home, k, peer):
        return pltpu.make_async_remote_copy(
            src_ref=tile,
            dst_ref=tbuf.at[home],
            send_sem=t_send.at[k],
            recv_sem=t_recv.at[home],
            device_id=peer,
            device_id_type=MESH,
        )

    first = []
    for dy in row_steps:
        first.append(send(own_tile, (REACH - dy, x), len(first), chip(0, dy)))
    for dx in (1, 3, 2):
        first.append(send(own_tile, (REACH, x), len(first), chip(dx, 0)))
    for copy in first:
        copy.start()

    shares = []
    for k, (src, dst) in enumerate(
        (
            (nbr_hbm.at[0], nbr_s.at[c]),
            (coup_hbm.at[0], coup_s.at[c]),
            (inter_hbm.at[0], sbuf.at[pl.ds(c * slots, slots)]),
        )
    ):
        shares.append(
            pltpu.make_async_remote_copy(
                src_ref=src, dst_ref=dst, send_sem=s_send.at[k], recv_sem=s_recv.at[k],
                device_id=sibling, device_id_type=MESH,
            )
        )
    for copy in shares:
        copy.start()

    for k in (4, 2, 3, 5, 6, 7):
        loads[k].wait()
    acc[...] = lax.dot_general(
        fbuf[0], fbuf[1], (((0,), (0,)), ((), ())), preferred_element_type=jnp.float32
    )
    for copy in shares:
        copy.wait()

    for r in range(2 * REACH + 1):
        for xs in range(RING):
            q = far_row(r - REACH) * RING + xs
            slot = jnp.int32(0)
            factor = jnp.float32(0)
            for core in range(2):
                for n in range(slots):
                    hit = nbr_s[core, n] == q
                    slot = jnp.where(hit, core * slots + n, slot)
                    factor = jnp.where(hit, coup_s[core, n], factor)
            slot_s[r, xs] = slot
            factor_s[r, xs] = factor

    def arrived(r, xs):
        tile = tbuf.at[r, xs]
        pltpu.make_async_copy(tile, tile, t_recv.at[r, xs]).wait()

    def wanted(r, source, dest):
        if r == 0:
            return dest < source
        if r == 2 * REACH:
            return dest > source
        return None

    def under(condition, act):
        if condition is None:
            act()
        else:
            pl.when(condition)(act)

    def relay_copies(r):
        base = len(first) + 3 * (r if r < REACH else r - 1)
        return [
            (wanted(r, x, column(dx)), send(tbuf.at[r, x], (r, x), base + k, chip(dx, 0)))
            for k, dx in enumerate((1, 3, 2))
        ]

    def relay(r):
        arrived(r, x)
        for condition, copy in relay_copies(r):
            under(condition, copy.start)

    def couple(r, xs):
        slot = slot_s[r, xs]
        near = sbuf[slot]
        half = jnp.dot(near, tbuf[r, xs], preferred_element_type=jnp.float32).astype(jnp.bfloat16)
        projected = lax.dot_general(
            half, sbuf[slot, :, cols], (((1,), (1,)), ((), ())), preferred_element_type=jnp.float32
        )
        acc[...] += factor_s[r, xs] * projected

    early = row < REACH

    def couple_row(r):
        if r != REACH:
            couple(r, x)

        @pl.loop(1, RING)
        def _(k):
            dx = jnp.where(k == 1, 1, jnp.where(k == 2, 3, 2))
            xs = column(dx)

            def act():
                arrived(r, xs)
                couple(r, xs)

            under(wanted(r, xs, x), act)

    relay(REACH + 1)
    relay(REACH + 2)

    @pl.when(jnp.logical_not(early))
    def _():
        relay(REACH - 1)
        relay(REACH - 2)

    couple(REACH, x)
    couple_row(REACH)
    couple_row(REACH + 1)
    couple_row(REACH + 2)

    @pl.when(early)
    def _():
        relay(REACH - 1)
        relay(REACH - 2)

    couple_row(REACH - 1)
    couple_row(REACH - 2)

    theirs = pl.ds(pl.multiple_of(other * half_w, half_w), half_w)
    send_half[...] = acc[theirs, :]
    ship = pltpu.make_async_remote_copy(
        src_ref=send_half, dst_ref=recv_half, send_sem=r_sem.at[0], recv_sem=r_sem.at[1],
        device_id=sibling, device_id_type=MESH,
    )
    ship.start()
    rows = lax.broadcasted_iota(jnp.int32, (half_w, width), 0) + c * half_w
    columns = lax.broadcasted_iota(jnp.int32, (half_w, width), 1)
    live = (rows < rank) & (columns < rank)
    by_row = jnp.transpose(jnp.broadcast_to(energy[:, cols], (half_w, half_w)))
    denominator = jnp.concatenate([by_row, by_row], axis=1) + energy[...]
    own = jnp.where(live, own_rows[...].astype(jnp.float32), 0.0)
    for copy in first:
        copy.wait_send()
    for r in (REACH + 1, REACH + 2, REACH - 1, REACH - 2):
        for condition, copy in relay_copies(r):
            under(condition, copy.wait_send)
    ship.wait()
    summed = acc[cols, :] + recv_half[...]
    residual = jnp.where(live, summed + denominator * own, 0.0)
    res_ref[0] = residual
    upd_ref[0] = own - residual / denominator


def shards(amplitudes, ranks, neighbours, intersections, couplings, energies, factors):
    pairs = lax.axis_size("pair")
    width = amplitudes.shape[1]
    half_w = width // 2
    slots = neighbours.shape[1]
    span = factors.shape[2]
    out = jax.ShapeDtypeStruct((1, half_w, width), jnp.float32)
    hbm = pl.BlockSpec(memory_space=pltpu.HBM)
    vmem = pl.BlockSpec(memory_space=pltpu.VMEM)
    dma = pltpu.SemaphoreType.DMA
    tiles = (2 * REACH + 1, RING)
    return pl.pallas_call(
        functools.partial(body, pairs),
        out_shape=(out, out),
        in_specs=[hbm] * 7,
        out_specs=(vmem, vmem),
        scratch_shapes=[
            pltpu.VMEM(tiles + (width, half_w), jnp.bfloat16),
            pltpu.VMEM((2 * slots, width, width), jnp.bfloat16),
            pltpu.VMEM((2, span, width), jnp.bfloat16),
            pltpu.VMEM((width, width), jnp.float32),
            pltpu.VMEM((half_w, width), jnp.float32),
            pltpu.VMEM((half_w, width), jnp.float32),
            pltpu.VMEM((half_w, width), jnp.bfloat16),
            pltpu.VMEM((1, width), jnp.float32),
            pltpu.SMEM((1,), jnp.int32),
            pltpu.SMEM((2, slots), jnp.int32),
            pltpu.SMEM((2, slots), jnp.float32),
            pltpu.SMEM(tiles, jnp.int32),
            pltpu.SMEM(tiles, jnp.float32),
            dma((8,)),
            dma((3,)),
            dma((3,)),
            dma((7 + 3 * 2 * REACH,)),
            dma(tiles),
            dma((2,)),
        ],
        compiler_params=pltpu.CompilerParams(
            collective_id=0, has_side_effects=True, vmem_limit_bytes=VMEM_LIMIT
        ),
    )(amplitudes, ranks, neighbours, intersections, couplings, energies, factors)


VMEM_LIMIT = 56000000


def solution(mesh):
    return jax.shard_map(
        shards,
        mesh=mesh,
        in_specs=(
            P("pair", None, None),
            P("pair"),
            P("pair", "aux"),
            P("pair", "aux", None, None),
            P("pair", "aux"),
            P("pair", None),
            P("pair", None, "aux", None),
        ),
        out_specs=(P("pair", "aux", None), P("pair", "aux", None)),
        check_vma=False,
    )
```

```python
import functools

import jax
import jax.numpy as jnp
from jax import lax
from jax.experimental import pallas as pl
from jax.experimental.pallas import tpu as pltpu
from jax.sharding import PartitionSpec as P

WIN = 8
RING = 4
REACH = WIN // RING
MESH = pl.DeviceIdType.MESH


def body(
    pairs,
    amp_hbm,
    ranks_hbm,
    nbr_hbm,
    inter_hbm,
    coup_hbm,
    energy_hbm,
    fact_hbm,
    res_ref,
    upd_ref,
    tbuf,
    sbuf,
    fbuf,
    acc,
    send_half,
    recv_half,
    own_rows,
    energy,
    nbr_s,
    coup_s,
    slot_s,
    factor_s,
    loc_sem,
    s_send,
    s_recv,
    t_send,
    t_recv,
    r_sem,
    hello,
):
    width = amp_hbm.shape[1]
    half_w = width // 2
    slots = nbr_hbm.shape[1]
    rows_all = pairs // RING
    p = lax.axis_index("pair")
    c = lax.axis_index("aux")
    other = 1 - c
    sibling = (p, other)
    x = lax.rem(p, RING)
    row = p // RING
    cols = pl.ds(pl.multiple_of(c * half_w, half_w), half_w)

    def column(dx):
        return lax.rem(x + dx + RING, RING)

    def far_row(dy):
        return lax.rem(row + dy + rows_all, rows_all)

    def chip(dx, dy):
        return (far_row(dy) * RING + column(dx), c)

    def local(src, dst, k):
        return pltpu.make_async_copy(src, dst, loc_sem.at[k])

    own_tile = tbuf.at[REACH, x]
    loads = [
        local(energy_hbm, energy, 0),
        local(amp_hbm.at[0, :, cols], own_tile, 1),
        local(nbr_hbm.at[0], nbr_s.at[c], 2),
        local(coup_hbm.at[0], coup_s.at[c], 3),
        local(fact_hbm.at[0], fbuf, 4),
        local(inter_hbm.at[0], sbuf.at[pl.ds(c * slots, slots)], 5),
        local(amp_hbm.at[0, cols, :], own_rows, 6),
    ]
    for copy in loads:
        copy.start()

    barrier = pltpu.get_barrier_semaphore()
    callers = [sibling, chip(0, -1), chip(0, -2)]
    callers += [chip(dx, 0) for dx in (1, 2, 3)]
    for peer in callers:
        pl.semaphore_signal(barrier, inc=1, device_id=peer, device_id_type=MESH)

    loads[1].wait()
    rank = ranks_hbm[0]
    row_id = lax.broadcasted_iota(jnp.int32, (width, half_w), 0)
    col_id = lax.broadcasted_iota(jnp.int32, (width, half_w), 1) + c * half_w
    own_tile[...] = jnp.where(
        (row_id < rank) & (col_id < rank), own_tile[...].astype(jnp.float32), 0.0
    ).astype(jnp.bfloat16)

    pl.semaphore_wait(barrier, len(callers))

    def send(tile, home, k, peer):
        return pltpu.make_async_remote_copy(
            src_ref=tile,
            dst_ref=tbuf.at[home],
            send_sem=t_send.at[k],
            recv_sem=t_recv.at[home],
            device_id=peer,
            device_id_type=MESH,
        )

    up = [send(own_tile, (REACH - dy, x), dy - 1, chip(0, dy)) for dy in (1, 2)]
    down = [send(own_tile, (REACH + dy, x), 1 + dy, chip(0, -dy)) for dy in (1, 2)]
    side = [send(own_tile, (REACH, x), 3 + dx, chip(dx, 0)) for dx in (1, 3, 2)]
    first = up + side + down
    for copy in up:
        copy.start()
    for dy in (1, 2):
        pl.semaphore_signal(hello.at[dy - 1], inc=1, device_id=chip(0, dy), device_id_type=MESH)
    for copy in side:
        copy.start()

    def send_down(dy):
        pl.semaphore_wait(hello.at[dy - 1], 1)
        down[dy - 1].start()

    shares = []
    for k, (src, dst) in enumerate(
        (
            (nbr_hbm.at[0], nbr_s.at[c]),
            (coup_hbm.at[0], coup_s.at[c]),
            (inter_hbm.at[0], sbuf.at[pl.ds(c * slots, slots)]),
        )
    ):
        shares.append(
            pltpu.make_async_remote_copy(
                src_ref=src, dst_ref=dst, send_sem=s_send.at[k], recv_sem=s_recv.at[k],
                device_id=sibling, device_id_type=MESH,
            )
        )
    for copy in shares:
        copy.start()

    for k in (4, 2, 3, 5, 6, 0):
        loads[k].wait()
    acc[...] = lax.dot_general(
        fbuf[0], fbuf[1], (((0,), (0,)), ((), ())), preferred_element_type=jnp.float32
    )

    late = [row < dy for dy in (1, 2)]
    for dy in (1, 2):
        pl.when(jnp.logical_not(late[dy - 1]))(functools.partial(send_down, dy))
    for copy in shares:
        copy.wait()

    for r in range(2 * REACH + 1):
        for xs in range(RING):
            q = far_row(r - REACH) * RING + xs
            slot = jnp.int32(0)
            factor = jnp.float32(0)
            for core in range(2):
                for n in range(slots):
                    hit = nbr_s[core, n] == q
                    slot = jnp.where(hit, core * slots + n, slot)
                    factor = jnp.where(hit, coup_s[core, n], factor)
            slot_s[r, xs] = slot
            factor_s[r, xs] = factor

    def arrived(r, xs):
        tile = tbuf.at[r, xs]
        pltpu.make_async_copy(tile, tile, t_recv.at[r, xs]).wait()

    def wanted(r, source, dest):
        if r == 0:
            return dest < source
        if r == 2 * REACH:
            return dest > source
        return None

    def under(condition, act):
        if condition is None:
            act()
        else:
            pl.when(condition)(act)

    def relay_copies(r):
        base = 7 + 3 * (r if r < REACH else r - 1)
        return [
            (wanted(r, x, column(dx)), send(tbuf.at[r, x], (r, x), base + k, chip(dx, 0)))
            for k, dx in enumerate((1, 3, 2))
        ]

    def relay(r):
        arrived(r, x)
        for condition, copy in relay_copies(r):
            under(condition, copy.start)

    def couple(r, xs):
        slot = slot_s[r, xs]
        near = sbuf[slot]
        half = jnp.dot(near, tbuf[r, xs], preferred_element_type=jnp.float32).astype(jnp.bfloat16)
        projected = lax.dot_general(
            half, sbuf[slot, :, cols], (((1,), (1,)), ((), ())), preferred_element_type=jnp.float32
        )
        acc[...] += factor_s[r, xs] * projected

    def couple_row(r):
        if r != REACH:
            couple(r, x)

        @pl.loop(1, RING)
        def _(k):
            dx = jnp.where(k == 1, 1, jnp.where(k == 2, 3, 2))
            xs = column(dx)

            def act():
                arrived(r, xs)
                couple(r, xs)

            under(wanted(r, xs, x), act)

    relay(REACH + 1)
    relay(REACH + 2)

    for dy in (1, 2):
        pl.when(jnp.logical_not(late[dy - 1]))(functools.partial(relay, REACH - dy))

    couple(REACH, x)
    couple_row(REACH)
    couple_row(REACH + 1)
    couple_row(REACH + 2)

    for dy in (1, 2):
        pl.when(late[dy - 1])(functools.partial(send_down, dy))
    for dy in (1, 2):
        pl.when(late[dy - 1])(functools.partial(relay, REACH - dy))

    couple_row(REACH - 1)
    couple_row(REACH - 2)

    theirs = pl.ds(pl.multiple_of(other * half_w, half_w), half_w)
    send_half[...] = acc[theirs, :]
    ship = pltpu.make_async_remote_copy(
        src_ref=send_half, dst_ref=recv_half, send_sem=r_sem.at[0], recv_sem=r_sem.at[1],
        device_id=sibling, device_id_type=MESH,
    )
    ship.start()
    rows = lax.broadcasted_iota(jnp.int32, (half_w, width), 0) + c * half_w
    columns = lax.broadcasted_iota(jnp.int32, (half_w, width), 1)
    live = (rows < rank) & (columns < rank)
    by_row = jnp.transpose(jnp.broadcast_to(energy[:, cols], (half_w, half_w)))
    denominator = jnp.concatenate([by_row, by_row], axis=1) + energy[...]
    own = jnp.where(live, own_rows[...].astype(jnp.float32), 0.0)
    for copy in first:
        copy.wait_send()
    for r in (REACH + 1, REACH + 2, REACH - 1, REACH - 2):
        for condition, copy in relay_copies(r):
            under(condition, copy.wait_send)
    ship.wait()
    summed = acc[cols, :] + recv_half[...]
    residual = jnp.where(live, summed + denominator * own, 0.0)
    res_ref[0] = residual
    upd_ref[0] = own - residual / denominator


def store(res_ref, upd_ref, res_hbm, upd_hbm, sem):
    copies = [
        pltpu.make_async_copy(src, dst, sem.at[k])
        for k, (src, dst) in enumerate(((res_ref, res_hbm), (upd_ref, upd_hbm)))
    ]
    for copy in copies:
        copy.start()
    for copy in copies:
        copy.wait()


def shards(amplitudes, ranks, neighbours, intersections, couplings, energies, factors):
    pairs = lax.axis_size("pair")
    width = amplitudes.shape[1]
    half_w = width // 2
    slots = neighbours.shape[1]
    span = factors.shape[2]
    out = jax.ShapeDtypeStruct((1, half_w, width), jnp.float32)
    hbm = pl.BlockSpec(memory_space=pltpu.HBM)
    vmem = pl.BlockSpec(memory_space=pltpu.VMEM)
    dma = pltpu.SemaphoreType.DMA
    tiles = (2 * REACH + 1, RING)
    results = pl.pallas_call(
        functools.partial(body, pairs),
        out_shape=(out, out),
        in_specs=[hbm, pl.BlockSpec(memory_space=pltpu.SMEM)] + [hbm] * 5,
        out_specs=(vmem, vmem),
        scratch_shapes=[
            pltpu.VMEM(tiles + (width, half_w), jnp.bfloat16),
            pltpu.VMEM((2 * slots, width, width), jnp.bfloat16),
            pltpu.VMEM((2, span, width), jnp.bfloat16),
            pltpu.VMEM((width, width), jnp.float32),
            pltpu.VMEM((half_w, width), jnp.float32),
            pltpu.VMEM((half_w, width), jnp.float32),
            pltpu.VMEM((half_w, width), jnp.bfloat16),
            pltpu.VMEM((1, width), jnp.float32),
            pltpu.SMEM((2, slots), jnp.int32),
            pltpu.SMEM((2, slots), jnp.float32),
            pltpu.SMEM(tiles, jnp.int32),
            pltpu.SMEM(tiles, jnp.float32),
            dma((7,)),
            dma((3,)),
            dma((3,)),
            dma((7 + 3 * 2 * REACH,)),
            dma(tiles),
            dma((2,)),
            pltpu.SemaphoreType.REGULAR((2,)),
        ],
        compiler_params=pltpu.CompilerParams(
            collective_id=0, has_side_effects=True, vmem_limit_bytes=VMEM_LIMIT
        ),
    )(*[a if a.ndim == 1 else pltpu.with_memory_space_constraint(a, pltpu.HBM) for a in (amplitudes, ranks, neighbours, intersections, couplings, energies, factors)])

    return pl.pallas_call(
        store,
        out_shape=(out, out),
        in_specs=[vmem, vmem],
        out_specs=(hbm, hbm),
        scratch_shapes=[dma((2,))],
        compiler_params=pltpu.CompilerParams(vmem_limit_bytes=1 << 20),
    )(*results)


VMEM_LIMIT = 12000000


def solution(mesh):
    return jax.shard_map(
        shards,
        mesh=mesh,
        in_specs=(
            P("pair", None, None),
            P("pair"),
            P("pair", "aux"),
            P("pair", "aux", None, None),
            P("pair", "aux"),
            P("pair", None),
            P("pair", None, "aux", None),
        ),
        out_specs=(P("pair", "aux", None), P("pair", "aux", None)),
        check_vma=False,
    )
```

```python
import functools

import jax
import jax.numpy as jnp
from jax import lax
from jax.experimental import pallas as pl
from jax.experimental.pallas import tpu as pltpu
from jax.sharding import PartitionSpec as P

WIN = 8
RING = 4
REACH = WIN // RING
PIECES = 2
MESH = pl.DeviceIdType.MESH


def body(
    pairs,
    amp_hbm,
    ranks_hbm,
    nbr_hbm,
    inter_hbm,
    coup_hbm,
    energy_hbm,
    fact_hbm,
    res_ref,
    upd_ref,
    tbuf,
    sbuf,
    fbuf,
    acc,
    send_half,
    recv_half,
    own_rows,
    energy,
    nbr_s,
    coup_s,
    slot_s,
    factor_s,
    loc_sem,
    s_send,
    s_recv,
    t_send,
    t_recv,
    r_sem,
    hello,
):
    width = amp_hbm.shape[1]
    half_w = width // 2
    slots = nbr_hbm.shape[1]
    rows_all = pairs // RING
    p = lax.axis_index("pair")
    c = lax.axis_index("aux")
    other = 1 - c
    sibling = (p, other)
    x = lax.rem(p, RING)
    row = p // RING
    cols = pl.ds(pl.multiple_of(c * half_w, half_w), half_w)

    def column(dx):
        return lax.rem(x + dx + RING, RING)

    def far_row(dy):
        return lax.rem(row + dy + rows_all, rows_all)

    def chip(dx, dy):
        return (far_row(dy) * RING + column(dx), c)

    def local(src, dst, k):
        return pltpu.make_async_copy(src, dst, loc_sem.at[k])

    own_tile = tbuf.at[REACH, x]
    loads = [
        local(energy_hbm, energy, 0),
        local(amp_hbm.at[0, :, cols], own_tile, 1),
        local(nbr_hbm.at[0], nbr_s.at[c], 2),
        local(coup_hbm.at[0], coup_s.at[c], 3),
        local(fact_hbm.at[0], fbuf, 4),
        local(inter_hbm.at[0], sbuf.at[pl.ds(c * slots, slots)], 5),
        local(amp_hbm.at[0, cols, :], own_rows, 6),
    ]
    for copy in loads:
        copy.start()

    barrier = pltpu.get_barrier_semaphore()
    callers = [sibling, chip(0, -1), chip(0, -2)]
    callers += [chip(dx, 0) for dx in (1, 2, 3)]
    for peer in callers:
        pl.semaphore_signal(barrier, inc=1, device_id=peer, device_id_type=MESH)

    loads[1].wait()
    rank = ranks_hbm[0]
    row_id = lax.broadcasted_iota(jnp.int32, (width, half_w), 0)
    col_id = lax.broadcasted_iota(jnp.int32, (width, half_w), 1) + c * half_w
    own_tile[...] = jnp.where(
        (row_id < rank) & (col_id < rank), own_tile[...].astype(jnp.float32), 0.0
    ).astype(jnp.bfloat16)

    pl.semaphore_wait(barrier, len(callers))

    def piece(r, xs, h):
        return tbuf.at[r, xs, pl.ds(h * (width // PIECES), width // PIECES)]

    def send(r, xs, home, k, peer):
        return [
            pltpu.make_async_remote_copy(
                src_ref=piece(r, xs, h),
                dst_ref=piece(home, xs, h),
                send_sem=t_send.at[k, h],
                recv_sem=t_recv.at[home, xs, h],
                device_id=peer,
                device_id_type=MESH,
            )
            for h in range(PIECES)
        ]

    def start(copies):
        for copy in copies:
            copy.start()

    top = rows_all - 1
    across = column(2)
    lead = jnp.where(row == top, 1, 2)
    up = [send(REACH, x, REACH - dy, dy - 1, chip(0, dy)) for dy in (lead, 3 - lead)]
    down = [send(REACH, x, REACH + dy, 1 + dy, chip(0, -dy)) for dy in (1, 2)]
    side = [send(REACH, x, REACH, 3 + dx, chip(dx, 0)) for dx in (2, 1, 3)]
    pass_up = send(REACH, across, REACH - 1, 7, chip(0, 1))
    pass_down = send(REACH, across, REACH + 1, 8, chip(0, -1))
    first = up + side + down + [pass_up, pass_down]
    for copies in up:
        start(copies)
    for dy in (1, 2):
        pl.semaphore_signal(hello.at[dy - 1], inc=1, device_id=chip(0, dy), device_id_type=MESH)
    for copies in side:
        start(copies)

    def send_down(dy):
        pl.semaphore_wait(hello.at[dy - 1], 1)
        start(down[dy - 1])

    shares = []
    for k, (src, dst) in enumerate(
        (
            (nbr_hbm.at[0], nbr_s.at[c]),
            (coup_hbm.at[0], coup_s.at[c]),
            (inter_hbm.at[0], sbuf.at[pl.ds(c * slots, slots)]),
        )
    ):
        shares.append(
            pltpu.make_async_remote_copy(
                src_ref=src, dst_ref=dst, send_sem=s_send.at[k], recv_sem=s_recv.at[k],
                device_id=sibling, device_id_type=MESH,
            )
        )
    for copy in shares:
        copy.start()

    for k in (4, 2, 3, 5, 6, 0):
        loads[k].wait()
    acc[...] = lax.dot_general(
        fbuf[0], fbuf[1], (((0,), (0,)), ((), ())), preferred_element_type=jnp.float32
    )

    side_of = jnp.where(row < REACH, 1, -1)

    def late(dy):
        low = (row < dy) & ((row > 0) | (c == 1))
        return low | (top - row < dy)

    def soon(dy):
        return jnp.logical_not(late(dy))

    for dy in (1, 2):
        pl.when(jnp.logical_not(row < dy))(functools.partial(send_down, dy))
    for copy in shares:
        copy.wait()

    for r in range(2 * REACH + 1):
        for xs in range(RING):
            q = far_row(r - REACH) * RING + xs
            slot = jnp.int32(0)
            factor = jnp.float32(0)
            for core in range(2):
                for n in range(slots):
                    hit = nbr_s[core, n] == q
                    slot = jnp.where(hit, core * slots + n, slot)
                    factor = jnp.where(hit, coup_s[core, n], factor)
            slot_s[r, xs] = slot
            factor_s[r, xs] = factor

    def arrived(r, xs, pieces=range(PIECES)):
        for h in pieces:
            part = piece(r, xs, h)
            pltpu.make_async_copy(part, part, t_recv.at[r, xs, h]).wait()

    def wanted(r, source, dest):
        return ((r > 0) | (dest <= source)) & ((r < 2 * REACH) | (dest >= source))

    def relay_copies(r):
        outer = (r == 0) | (r == 2 * REACH)
        copies = []
        for k, dx in enumerate((2, 1, 3)):
            needed = wanted(r, x, column(dx))
            if dx == 2:
                needed &= outer
            copies.append((needed, send(r, x, r, 9 + 3 * r + k, chip(dx, 0))))
        return copies

    def relay(r):
        copies = relay_copies(r)
        for h in range(PIECES):
            arrived(r, x, (h,))
            for needed, parts in copies:
                pl.when(needed)(parts[h].start)

    def couple_row(r):
        picks = []
        for dx in (0, 1, 3, 2):
            xs = column(dx)
            if dx == 0:
                picks.append((xs, factor_s[r, xs]))
            else:
                needed = wanted(r, xs, x)
                due = needed & (r != REACH) if dx == 2 else needed
                pl.when(due)(functools.partial(arrived, r, xs))
                picks.append((jnp.where(needed, xs, x), jnp.where(needed, factor_s[r, xs], 0.0)))
        total = acc[...]
        for xs, factor in picks:
            slot = slot_s[r, xs]
            half = jnp.dot(
                sbuf[slot], tbuf[r, xs], preferred_element_type=jnp.float32
            ).astype(jnp.bfloat16)
            total += factor * lax.dot_general(
                half, sbuf[slot, :, cols], (((1,), (1,)), ((), ())), preferred_element_type=jnp.float32
            )
        acc[...] = total

    arrived(REACH, across)
    start(pass_up)
    pl.when(row > 0)(functools.partial(start, pass_down))
    for dy in (1, 2):
        relay(REACH + dy * side_of)

    def other_side(dy):
        def release():
            send_down(dy)
            if dy == 1:
                start(pass_down)

        pl.when(row < dy)(release)
        relay(REACH - dy * side_of)

    for dy in (1, 2):
        pl.when(soon(dy))(functools.partial(other_side, dy))

    @pl.loop(0, REACH + 1)
    def _(k):
        couple_row(REACH + k * side_of)

    for dy in (1, 2):
        pl.when(late(dy))(functools.partial(other_side, dy))

    @pl.loop(1, REACH + 1)
    def _(k):
        couple_row(REACH - k * side_of)

    theirs = pl.ds(pl.multiple_of(other * half_w, half_w), half_w)
    send_half[...] = acc[theirs, :]
    ship = pltpu.make_async_remote_copy(
        src_ref=send_half, dst_ref=recv_half, send_sem=r_sem.at[0], recv_sem=r_sem.at[1],
        device_id=sibling, device_id_type=MESH,
    )
    ship.start()
    rows = lax.broadcasted_iota(jnp.int32, (half_w, width), 0) + c * half_w
    columns = lax.broadcasted_iota(jnp.int32, (half_w, width), 1)
    live = (rows < rank) & (columns < rank)
    by_row = jnp.transpose(jnp.broadcast_to(energy[:, cols], (half_w, half_w)))
    denominator = jnp.concatenate([by_row, by_row], axis=1) + energy[...]
    own = jnp.where(live, own_rows[...].astype(jnp.float32), 0.0)
    for copies in first:
        for copy in copies:
            copy.wait_send()

    @pl.loop(0, 2 * REACH + 1)
    def _(r):
        for needed, copies in relay_copies(r):
            @pl.when(needed & (r != REACH))
            def _(copies=copies):
                for copy in copies:
                    copy.wait_send()

    ship.wait()
    summed = acc[cols, :] + recv_half[...]
    residual = jnp.where(live, summed + denominator * own, 0.0)
    res_ref[0] = residual
    upd_ref[0] = own - residual / denominator


def store(res_ref, upd_ref, res_hbm, upd_hbm, sem):
    copies = [
        pltpu.make_async_copy(src, dst, sem.at[k])
        for k, (src, dst) in enumerate(((res_ref, res_hbm), (upd_ref, upd_hbm)))
    ]
    for copy in copies:
        copy.start()
    for copy in copies:
        copy.wait()


def shards(amplitudes, ranks, neighbours, intersections, couplings, energies, factors):
    pairs = lax.axis_size("pair")
    width = amplitudes.shape[1]
    half_w = width // 2
    slots = neighbours.shape[1]
    span = factors.shape[2]
    out = jax.ShapeDtypeStruct((1, half_w, width), jnp.float32)
    hbm = pl.BlockSpec(memory_space=pltpu.HBM)
    vmem = pl.BlockSpec(memory_space=pltpu.VMEM)
    dma = pltpu.SemaphoreType.DMA
    tiles = (2 * REACH + 1, RING)
    results = pl.pallas_call(
        functools.partial(body, pairs),
        out_shape=(out, out),
        in_specs=[hbm, pl.BlockSpec(memory_space=pltpu.SMEM)] + [hbm] * 5,
        out_specs=(vmem, vmem),
        scratch_shapes=[
            pltpu.VMEM(tiles + (width, half_w), jnp.bfloat16),
            pltpu.VMEM((2 * slots, width, width), jnp.bfloat16),
            pltpu.VMEM((2, span, width), jnp.bfloat16),
            pltpu.VMEM((width, width), jnp.float32),
            pltpu.VMEM((half_w, width), jnp.float32),
            pltpu.VMEM((half_w, width), jnp.float32),
            pltpu.VMEM((half_w, width), jnp.bfloat16),
            pltpu.VMEM((1, width), jnp.float32),
            pltpu.SMEM((2, slots), jnp.int32),
            pltpu.SMEM((2, slots), jnp.float32),
            pltpu.SMEM(tiles, jnp.int32),
            pltpu.SMEM(tiles, jnp.float32),
            dma((7,)),
            dma((3,)),
            dma((3,)),
            dma((9 + 3 * (2 * REACH + 1), PIECES)),
            dma(tiles + (PIECES,)),
            dma((2,)),
            pltpu.SemaphoreType.REGULAR((2,)),
        ],
        compiler_params=pltpu.CompilerParams(
            collective_id=0, has_side_effects=True, vmem_limit_bytes=VMEM_LIMIT
        ),
    )(*[a if a.ndim == 1 else pltpu.with_memory_space_constraint(a, pltpu.HBM) for a in (amplitudes, ranks, neighbours, intersections, couplings, energies, factors)])

    return pl.pallas_call(
        store,
        out_shape=(out, out),
        in_specs=[vmem, vmem],
        out_specs=(hbm, hbm),
        scratch_shapes=[dma((2,))],
        compiler_params=pltpu.CompilerParams(vmem_limit_bytes=1 << 20),
    )(*results)


VMEM_LIMIT = 12000000


def solution(mesh):
    return jax.shard_map(
        shards,
        mesh=mesh,
        in_specs=(
            P("pair", None, None),
            P("pair"),
            P("pair", "aux"),
            P("pair", "aux", None, None),
            P("pair", "aux"),
            P("pair", None),
            P("pair", None, "aux", None),
        ),
        out_specs=(P("pair", "aux", None), P("pair", "aux", None)),
        check_vma=False,
    )
```

```python
import functools

import jax
import jax.numpy as jnp
from jax import lax
from jax.experimental import pallas as pl
from jax.experimental.pallas import tpu as pltpu
from jax.sharding import PartitionSpec as P

WIN = 8
RING = 4
REACH = WIN // RING
PIECES = 2
MESH = pl.DeviceIdType.MESH


def body(
    pairs,
    amp_hbm,
    ranks_smem,
    nbr_hbm,
    inter_hbm,
    coup_hbm,
    energy_hbm,
    fact_hbm,
    res_ref,
    upd_ref,
    tbuf,
    sbuf,
    fbuf,
    acc,
    send_half,
    recv_half,
    own_rows,
    energy,
    nbr_s,
    coup_s,
    loc_sem,
    s_send,
    s_recv,
    t_send,
    t_recv,
    r_sem,
    hello,
):
    width = amp_hbm.shape[1]
    half_w = width // 2
    slots = nbr_hbm.shape[1]
    rows_all = pairs // RING
    p = lax.axis_index("pair")
    c = lax.axis_index("aux")
    other = 1 - c
    sibling = (p, other)
    x = lax.rem(p, RING)
    row = p // RING
    cols = pl.ds(pl.multiple_of(c * half_w, half_w), half_w)

    def column(dx):
        return lax.rem(x + dx + RING, RING)

    def far_row(dy):
        return lax.rem(row + dy + rows_all, rows_all)

    def chip(dx, dy):
        return (far_row(dy) * RING + column(dx), c)

    def local(src, dst, k):
        return pltpu.make_async_copy(src, dst, loc_sem.at[k])

    own_tile = tbuf.at[REACH, x]
    loads = [
        local(amp_hbm.at[0, :, cols], own_tile, 1),
        local(energy_hbm, energy, 0),
        local(nbr_hbm.at[0], nbr_s.at[c], 2),
        local(coup_hbm.at[0], coup_s.at[c], 3),
        local(fact_hbm.at[0], fbuf, 4),
        local(inter_hbm.at[0], sbuf.at[pl.ds(c * slots, slots)], 5),
        local(amp_hbm.at[0, cols, :], own_rows, 6),
    ]
    loads[0].start()

    barrier = pltpu.get_barrier_semaphore()
    even = lax.rem(row, 2) == 0

    def greet(sem, peer):
        pl.semaphore_signal(sem, inc=1, device_id=peer, device_id_type=MESH)

    pl.when(even)(lambda: greet(barrier, chip(0, -2)))
    callers = [chip(dx, 0) for dx in (2, 1, 3)] + [chip(0, -1), sibling]
    for peer in callers:
        greet(barrier, peer)
    for copy in loads[1:]:
        copy.start()

    loads[0].wait()
    rank = ranks_smem[0]
    row_id = lax.broadcasted_iota(jnp.int32, (width, half_w), 0)
    col_id = lax.broadcasted_iota(jnp.int32, (width, half_w), 1) + c * half_w
    own_tile[...] = jnp.where(
        (row_id < rank) & (col_id < rank), own_tile[...].astype(jnp.float32), 0.0
    ).astype(jnp.bfloat16)

    pl.semaphore_wait(barrier, len(callers) + jnp.where(even, 1, 0))

    def piece(r, xs, h):
        return tbuf.at[r, xs, pl.ds(h * (width // PIECES), width // PIECES)]

    def send(r, xs, home, k, peer):
        def copy(src, dst, recv_sem):
            return pltpu.make_async_remote_copy(
                src_ref=src, dst_ref=dst, send_sem=t_send.at[k], recv_sem=recv_sem,
                device_id=peer, device_id_type=MESH,
            )

        parts = [
            copy(piece(r, xs, h), piece(home, xs, h), t_recv.at[home, xs, h]) for h in range(PIECES)
        ]
        return parts, copy(tbuf.at[r, xs], tbuf.at[home, xs], t_recv.at[home, xs, 0])

    def start(copies):
        for copy in copies[0]:
            copy.start()

    def sent(group):
        for _, whole in group:
            whole.wait_send()

    top = rows_all - 1
    across = column(2)
    up = [send(REACH, x, REACH - dy, dy - 1, chip(0, dy)) for dy in (1, 2)]
    down = [send(REACH, x, REACH + dy, 1 + dy, chip(0, -dy)) for dy in (1, 2)]
    side = [send(REACH, x, REACH, 3 + dx, chip(dx, 0)) for dx in (2, 1, 3)]
    pass_up = send(REACH, across, REACH - 1, 7, chip(0, 1))
    pass_down = send(REACH, across, REACH + 1, 8, chip(0, -1))
    hand_up = send(REACH - 1, x, REACH - 2, 9, chip(0, 1))
    hand_down = send(REACH + 1, x, REACH + 2, 10, chip(0, -1))
    hand_two = send(REACH - 1, across, 0, 27, chip(0, 1))
    hands_two = (row == 0) & (across > x)
    always = up[:1] + side + down[:1] + [pass_up, pass_down]
    if_even = [up[1], down[1], hand_up, hand_down]
    pl.when(even)(lambda: start(up[1]))
    start(up[0])
    greet(hello.at[0], chip(0, 1))
    pl.when(even)(lambda: greet(hello.at[1], chip(0, 2)))
    for copies in side:
        start(copies)

    def send_down(dy):
        def act():
            pl.semaphore_wait(hello.at[dy - 1], 1)
            start(down[dy - 1])

        if dy == 2:
            pl.when(even)(act)
        else:
            act()

    shares = []
    for k, (src, dst) in enumerate(
        (
            (nbr_hbm.at[0], nbr_s.at[c]),
            (coup_hbm.at[0], coup_s.at[c]),
            (inter_hbm.at[0], sbuf.at[pl.ds(c * slots, slots)]),
        )
    ):
        shares.append(
            pltpu.make_async_remote_copy(
                src_ref=src, dst_ref=dst, send_sem=s_send.at[k], recv_sem=s_recv.at[k],
                device_id=sibling, device_id_type=MESH,
            )
        )
    for copy in shares:
        copy.start()

    for copy in loads[1:]:
        copy.wait()
    acc[...] = lax.dot_general(
        fbuf[0], fbuf[1], (((0,), (0,)), ((), ())), preferred_element_type=jnp.float32
    )

    side_of = jnp.where(row < REACH, 1, -1)

    def late(dy):
        low = (row < dy) & ((row > 0) | (c == 1))
        return low | (top - row < dy)

    def soon(dy):
        return jnp.logical_not(late(dy))

    for dy in (1, 2):
        pl.when(jnp.logical_not(row < dy))(functools.partial(send_down, dy))
    def arrived(r, xs, pieces=range(PIECES)):
        for h in pieces:
            part = piece(r, xs, h)
            pltpu.make_async_copy(part, part, t_recv.at[r, xs, h]).wait()

    def wanted(r, source, dest):
        return ((r > 0) | (dest <= source)) & ((r < 2 * REACH) | (dest >= source))

    def relay_copies(r):
        outer = ((r == 0) & (row != 1)) | (r == 2 * REACH)
        copies = []
        for k, dx in enumerate((2, 1, 3)):
            needed = wanted(r, x, column(dx))
            if dx == 2:
                needed &= outer
            copies.append((needed, send(r, x, r, 11 + 3 * r + k, chip(dx, 0))))
        return copies

    def relay(r):
        copies = relay_copies(r)
        for h in range(PIECES):
            arrived(r, x, (h,))
            pl.when(even & (r == REACH - 1))(hand_up[0][h].start)
            pl.when(even & (r == REACH + 1) & (row > 0))(hand_down[0][h].start)
            for needed, parts in copies:
                pl.when(needed)(parts[0][h].start)

    def entry_of(r, xs):
        q = far_row(r - REACH) * RING + xs
        core, at = jnp.int32(0), jnp.int32(0)
        for k in range(2):
            for n in range(slots):
                hit = nbr_s[k, n] == q
                core, at = jnp.where(hit, k, core), jnp.where(hit, n, at)
        return core * slots + at, jnp.where(nbr_s[core, at] == q, coup_s[core, at], 0.0)

    def picks_of(r):
        found = []
        for dx in (0, 1, 3, 2):
            xs = column(dx)
            needed = wanted(r, xs, x)
            slot, factor = entry_of(r, xs)
            found.append((jnp.where(needed, xs, x), slot, jnp.where(needed, factor, 0.0)))
        for dx in (1, 3, 2):
            xs = column(dx)
            due = wanted(r, xs, x)
            if dx == 2:
                due &= (r != REACH) & ((r != REACH - 1) | (row > 0))
            pl.when(due)(functools.partial(arrived, r, xs))
        return found

    def add_products(r, picks, span):
        total = acc[span, :]
        for xs, slot, factor in picks:
            half = jnp.dot(
                sbuf[slot, span, :], tbuf[r, xs], preferred_element_type=jnp.float32
            ).astype(jnp.bfloat16)
            total += factor * lax.dot_general(
                half, sbuf[slot, :, cols], (((1,), (1,)), ((), ())), preferred_element_type=jnp.float32
            )
        acc[span, :] = total

    def couple_row(r):
        add_products(r, picks_of(r), pl.ds(0, width))

    for h in range(PIECES):
        arrived(REACH, across, (h,))
        pass_up[0][h].start()
        pl.when(row > 0)(pass_down[0][h].start)
    for dy in (1, 2):
        relay(REACH + dy * side_of)

    def other_side(dy):
        def release():
            send_down(dy)
            if dy == 1:
                start(pass_down)
                start(hand_down)

        pl.when(row < dy)(release)
        relay(REACH - dy * side_of)

    for dy in (1, 2):
        pl.when(soon(dy))(functools.partial(other_side, dy))

    for copy in shares:
        copy.wait()

    @pl.loop(0, REACH + 1)
    def _(k):
        couple_row(REACH + k * side_of)

    for dy in (1, 2):
        pl.when(late(dy))(functools.partial(other_side, dy))

    @pl.when(row == 0)
    def _():
        for h in range(PIECES):
            arrived(REACH - 1, across, (h,))
            pl.when(hands_two)(hand_two[0][h].start)

    @pl.loop(1, REACH)
    def _(k):
        couple_row(REACH - k * side_of)

    theirs = pl.ds(pl.multiple_of(other * half_w, half_w), half_w)
    last = REACH - REACH * side_of
    picks = picks_of(last)
    add_products(last, picks, theirs)
    send_half[...] = acc[theirs, :]
    ship = pltpu.make_async_remote_copy(
        src_ref=send_half, dst_ref=recv_half, send_sem=r_sem.at[0], recv_sem=r_sem.at[1],
        device_id=sibling, device_id_type=MESH,
    )
    ship.start()
    add_products(last, picks, cols)
    rows = lax.broadcasted_iota(jnp.int32, (half_w, width), 0) + c * half_w
    columns = lax.broadcasted_iota(jnp.int32, (half_w, width), 1)
    live = (rows < rank) & (columns < rank)
    by_row = jnp.transpose(jnp.broadcast_to(energy[:, cols], (half_w, half_w)))
    denominator = jnp.concatenate([by_row, by_row], axis=1) + energy[...]
    own = jnp.where(live, own_rows[...].astype(jnp.float32), 0.0)
    sent(always)
    pl.when(even)(lambda: sent(if_even))
    pl.when(hands_two)(lambda: sent([hand_two]))

    @pl.loop(0, 2 * REACH + 1)
    def _(r):
        for needed, copies in relay_copies(r):
            pl.when(needed & (r != REACH))(functools.partial(sent, [copies]))

    here = acc[cols, :] + denominator * own
    ship.wait()
    residual = jnp.where(live, here + recv_half[...], 0.0)
    res_ref[0] = residual
    upd_ref[0] = own - residual / denominator


def store(res_ref, upd_ref, res_hbm, upd_hbm, sem):
    copies = [
        pltpu.make_async_copy(src, dst, sem.at[k])
        for k, (src, dst) in enumerate(((res_ref, res_hbm), (upd_ref, upd_hbm)))
    ]
    for copy in copies:
        copy.start()
    for copy in copies:
        copy.wait()


def shards(amplitudes, ranks, neighbours, intersections, couplings, energies, factors):
    pairs = lax.axis_size("pair")
    width = amplitudes.shape[1]
    half_w = width // 2
    slots = neighbours.shape[1]
    span = factors.shape[2]
    out = jax.ShapeDtypeStruct((1, half_w, width), jnp.float32)
    hbm = pl.BlockSpec(memory_space=pltpu.HBM)
    vmem = pl.BlockSpec(memory_space=pltpu.VMEM)
    dma = pltpu.SemaphoreType.DMA
    tiles = (2 * REACH + 1, RING)
    operands = [
        operand if operand.ndim == 1 else pltpu.with_memory_space_constraint(operand, pltpu.HBM)
        for operand in (amplitudes, ranks, neighbours, intersections, couplings, energies, factors)
    ]
    results = pl.pallas_call(
        functools.partial(body, pairs),
        out_shape=(out, out),
        in_specs=[hbm, pl.BlockSpec(memory_space=pltpu.SMEM)] + [hbm] * 5,
        out_specs=(vmem, vmem),
        scratch_shapes=[
            pltpu.VMEM(tiles + (width, half_w), jnp.bfloat16),
            pltpu.VMEM((2 * slots, width, width), jnp.bfloat16),
            pltpu.VMEM((2, span, width), jnp.bfloat16),
            pltpu.VMEM((width, width), jnp.float32),
            pltpu.VMEM((half_w, width), jnp.float32),
            pltpu.VMEM((half_w, width), jnp.float32),
            pltpu.VMEM((half_w, width), jnp.bfloat16),
            pltpu.VMEM((1, width), jnp.float32),
            pltpu.SMEM((2, slots), jnp.int32),
            pltpu.SMEM((2, slots), jnp.float32),
            dma((7,)),
            dma((3,)),
            dma((3,)),
            dma((13 + 3 * (2 * REACH + 1),)),
            dma(tiles + (PIECES,)),
            dma((2,)),
            pltpu.SemaphoreType.REGULAR((2,)),
        ],
        compiler_params=pltpu.CompilerParams(
            collective_id=0, has_side_effects=True, vmem_limit_bytes=VMEM_LIMIT
        ),
    )(*operands)
    return pl.pallas_call(
        store,
        out_shape=(out, out),
        in_specs=[vmem, vmem],
        out_specs=(hbm, hbm),
        scratch_shapes=[dma((2,))],
        compiler_params=pltpu.CompilerParams(vmem_limit_bytes=1 << 20),
    )(*results)


VMEM_LIMIT = 12000000


def solution(mesh):
    return jax.shard_map(
        shards,
        mesh=mesh,
        in_specs=(
            P("pair", None, None),
            P("pair"),
            P("pair", "aux"),
            P("pair", "aux", None, None),
            P("pair", "aux"),
            P("pair", None),
            P("pair", None, "aux", None),
        ),
        out_specs=(P("pair", "aux", None), P("pair", "aux", None)),
        check_vma=False,
    )
```

```python
import functools

import jax
import jax.numpy as jnp
from jax import lax
from jax.experimental import pallas as pl
from jax.experimental.pallas import tpu as pltpu
from jax.sharding import PartitionSpec as P

WIN = 8
RING = 4
REACH = WIN // RING
PIECES = 2
MESH = pl.DeviceIdType.MESH


def body(
    pairs,
    amp_hbm,
    ranks_smem,
    nbr_hbm,
    inter_hbm,
    coup_hbm,
    energy_hbm,
    fact_hbm,
    res_ref,
    upd_ref,
    tbuf,
    sbuf,
    fbuf,
    acc,
    send_half,
    recv_half,
    own_rows,
    energy,
    nbr_s,
    coup_s,
    loc_sem,
    s_send,
    s_recv,
    t_send,
    t_recv,
    r_sem,
    hello,
):
    width = amp_hbm.shape[1]
    half_w = width // 2
    slots = nbr_hbm.shape[1]
    rows_all = pairs // RING
    p = lax.axis_index("pair")
    c = lax.axis_index("aux")
    other = 1 - c
    sibling = (p, other)
    x = lax.rem(p, RING)
    row = p // RING
    cols = pl.ds(pl.multiple_of(c * half_w, half_w), half_w)

    def column(dx):
        return lax.rem(x + dx + RING, RING)

    def far_row(dy):
        return lax.rem(row + dy + rows_all, rows_all)

    def chip(dx, dy):
        return (far_row(dy) * RING + column(dx), c)

    def local(src, dst, k):
        return pltpu.make_async_copy(src, dst, loc_sem.at[k])

    own_tile = tbuf.at[REACH, x]
    loads = [
        local(amp_hbm.at[0, :, cols], own_tile, 1),
        local(energy_hbm, energy, 0),
        local(nbr_hbm.at[0], nbr_s.at[c], 2),
        local(coup_hbm.at[0], coup_s.at[c], 3),
        local(fact_hbm.at[0], fbuf, 4),
        local(inter_hbm.at[0], sbuf.at[pl.ds(c * slots, slots)], 5),
        local(amp_hbm.at[0, cols, :], own_rows, 6),
    ]
    loads[0].start()

    barrier = pltpu.get_barrier_semaphore()
    even = lax.rem(row, 2) == 0

    def greet(sem, peer):
        pl.semaphore_signal(sem, inc=1, device_id=peer, device_id_type=MESH)

    pl.when(even)(lambda: greet(barrier, chip(0, -2)))
    callers = [chip(dx, 0) for dx in (2, 1, 3)] + [chip(0, -1), sibling]
    for peer in callers:
        greet(barrier, peer)
    for copy in loads[1:]:
        copy.start()

    loads[0].wait()
    rank = ranks_smem[0]
    row_id = lax.broadcasted_iota(jnp.int32, (width, half_w), 0)
    col_id = lax.broadcasted_iota(jnp.int32, (width, half_w), 1) + c * half_w
    own_tile[...] = jnp.where(
        (row_id < rank) & (col_id < rank), own_tile[...].astype(jnp.float32), 0.0
    ).astype(jnp.bfloat16)

    pl.semaphore_wait(barrier, len(callers) + jnp.where(even, 1, 0))

    def piece(r, xs, h):
        return tbuf.at[r, xs, pl.ds(h * (width // PIECES), width // PIECES)]

    def send(r, xs, home, k, peer):
        def copy(src, dst, recv_sem):
            return pltpu.make_async_remote_copy(
                src_ref=src, dst_ref=dst, send_sem=t_send.at[k], recv_sem=recv_sem,
                device_id=peer, device_id_type=MESH,
            )

        parts = [
            copy(piece(r, xs, h), piece(home, xs, h), t_recv.at[home, xs, h]) for h in range(PIECES)
        ]
        return parts, copy(tbuf.at[r, xs], tbuf.at[home, xs], t_recv.at[home, xs, 0])

    def start(copies):
        for copy in copies[0]:
            copy.start()

    def sent(group):
        for _, whole in group:
            whole.wait_send()

    top = rows_all - 1
    across = column(2)
    up = [send(REACH, x, REACH - dy, dy - 1, chip(0, dy)) for dy in (1, 2)]
    down = [send(REACH, x, REACH + dy, 1 + dy, chip(0, -dy)) for dy in (1, 2)]
    side = [send(REACH, x, REACH, 3 + dx, chip(dx, 0)) for dx in (2, 1, 3)]
    pass_up = send(REACH, across, REACH - 1, 7, chip(0, 1))
    pass_down = send(REACH, across, REACH + 1, 8, chip(0, -1))
    hand_up = send(REACH - 1, x, REACH - 2, 9, chip(0, 1))
    hand_down = send(REACH + 1, x, REACH + 2, 10, chip(0, -1))
    hand_two = send(REACH - 1, across, 0, 27, chip(0, 1))
    hands_two = (row == 0) & (across > x)
    always = up[:1] + side + down[:1] + [pass_up, pass_down]
    if_even = [up[1], down[1], hand_up, hand_down]
    pl.when(even)(lambda: start(up[1]))
    start(up[0])
    greet(hello.at[0], chip(0, 1))
    pl.when(even)(lambda: greet(hello.at[1], chip(0, 2)))
    for copies in side:
        start(copies)

    def send_down(dy):
        def act():
            pl.semaphore_wait(hello.at[dy - 1], 1)
            start(down[dy - 1])

        if dy == 2:
            pl.when(even)(act)
        else:
            act()

    shares = []
    for k, (src, dst) in enumerate(
        (
            (nbr_hbm.at[0], nbr_s.at[c]),
            (coup_hbm.at[0], coup_s.at[c]),
            (inter_hbm.at[0], sbuf.at[pl.ds(c * slots, slots)]),
        )
    ):
        shares.append(
            pltpu.make_async_remote_copy(
                src_ref=src, dst_ref=dst, send_sem=s_send.at[k], recv_sem=s_recv.at[k],
                device_id=sibling, device_id_type=MESH,
            )
        )
    for copy in shares:
        copy.start()

    for copy in loads[1:]:
        copy.wait()
    acc[...] = lax.dot_general(
        fbuf[0], fbuf[1], (((0,), (0,)), ((), ())), preferred_element_type=jnp.float32
    )

    side_of = jnp.where(row < REACH, 1, -1)

    def late(dy):
        low = (row < dy) & ((row > 0) | (c == 1))
        return low | (top - row < dy)

    def soon(dy):
        return jnp.logical_not(late(dy))

    for dy in (1, 2):
        pl.when(jnp.logical_not(row < dy))(functools.partial(send_down, dy))
    def arrived(r, xs, pieces=range(PIECES)):
        for h in pieces:
            part = piece(r, xs, h)
            pltpu.make_async_copy(part, part, t_recv.at[r, xs, h]).wait()

    def wanted(r, source, dest):
        return ((r > 0) | (dest <= source)) & ((r < 2 * REACH) | (dest >= source))

    def relay_copies(r):
        outer = ((r == 0) & (row != 1)) | (r == 2 * REACH)
        copies = []
        for k, dx in enumerate((2, 1, 3)):
            needed = wanted(r, x, column(dx))
            if dx == 2:
                needed &= outer
            copies.append((needed, send(r, x, r, 11 + 3 * r + k, chip(dx, 0))))
        return copies

    def relay(r):
        copies = relay_copies(r)
        for h in range(PIECES):
            arrived(r, x, (h,))
            pl.when(even & (r == REACH - 1))(hand_up[0][h].start)
            pl.when(even & (r == REACH + 1) & (row > 0))(hand_down[0][h].start)
            for needed, parts in copies:
                pl.when(needed)(parts[0][h].start)

    def entry_of(r, xs):
        q = far_row(r - REACH) * RING + xs
        core, at = jnp.int32(0), jnp.int32(0)
        for k in range(2):
            for n in range(slots):
                hit = nbr_s[k, n] == q
                core, at = jnp.where(hit, k, core), jnp.where(hit, n, at)
        return core * slots + at, jnp.where(nbr_s[core, at] == q, coup_s[core, at], 0.0)

    def picks_of(r):
        found = []
        for dx in (0, 1, 3, 2):
            xs = column(dx)
            needed = wanted(r, xs, x)
            slot, factor = entry_of(r, xs)
            found.append((jnp.where(needed, xs, x), slot, jnp.where(needed, factor, 0.0)))
        for dx in (1, 3, 2):
            xs = column(dx)
            due = wanted(r, xs, x)
            if dx == 2:
                due &= (r != REACH) & ((r != REACH - 1) | (row > 0))
            pl.when(due)(functools.partial(arrived, r, xs))
        return found

    def add_products(r, picks, span):
        total = acc[span, :]
        for xs, slot, factor in picks:
            half = jnp.dot(
                sbuf[slot, span, :], tbuf[r, xs], preferred_element_type=jnp.float32
            ).astype(jnp.bfloat16)
            total += factor * lax.dot_general(
                half, sbuf[slot, :, cols], (((1,), (1,)), ((), ())), preferred_element_type=jnp.float32
            )
        return total

    def couple_row(r):
        acc[...] = add_products(r, picks_of(r), pl.ds(0, width))

    for h in range(PIECES):
        arrived(REACH, across, (h,))
        pass_up[0][h].start()
        pl.when(row > 0)(pass_down[0][h].start)
    for dy in (1, 2):
        relay(REACH + dy * side_of)

    def other_side(dy):
        def release():
            send_down(dy)
            if dy == 1:
                start(pass_down)
                start(hand_down)

        pl.when(row < dy)(release)
        relay(REACH - dy * side_of)

    for dy in (1, 2):
        pl.when(soon(dy))(functools.partial(other_side, dy))

    for copy in shares:
        copy.wait()

    def hand_across():
        for h in range(PIECES):
            arrived(REACH - 1, across, (h,))
            pl.when(hands_two)(hand_two[0][h].start)

    @pl.loop(0, REACH + 1)
    def _(k):
        couple_row(REACH + k * side_of)
        pl.when((row == 0) & (c == 0) & (k == 1))(hand_across)

    for dy in (1, 2):
        pl.when(late(dy))(functools.partial(other_side, dy))

    pl.when((row == 0) & (c == 1))(hand_across)

    @pl.loop(1, REACH)
    def _(k):
        couple_row(REACH - k * side_of)

    theirs = pl.ds(pl.multiple_of(other * half_w, half_w), half_w)
    last = REACH - REACH * side_of
    picks = picks_of(last)
    send_half[...] = add_products(last, picks, theirs)
    ship = pltpu.make_async_remote_copy(
        src_ref=send_half, dst_ref=recv_half, send_sem=r_sem.at[0], recv_sem=r_sem.at[1],
        device_id=sibling, device_id_type=MESH,
    )
    ship.start()
    mine = add_products(last, picks, cols)
    rows = lax.broadcasted_iota(jnp.int32, (half_w, width), 0) + c * half_w
    columns = lax.broadcasted_iota(jnp.int32, (half_w, width), 1)
    live = (rows < rank) & (columns < rank)
    by_row = jnp.transpose(jnp.broadcast_to(energy[:, cols], (half_w, half_w)))
    denominator = jnp.concatenate([by_row, by_row], axis=1) + energy[...]
    own = jnp.where(live, own_rows[...].astype(jnp.float32), 0.0)
    sent(always)
    pl.when(even)(lambda: sent(if_even))
    pl.when(hands_two)(lambda: sent([hand_two]))

    @pl.loop(0, 2 * REACH + 1)
    def _(r):
        for needed, copies in relay_copies(r):
            pl.when(needed & (r != REACH))(functools.partial(sent, [copies]))

    here = mine + denominator * own
    ship.wait()
    residual = jnp.where(live, here + recv_half[...], 0.0)
    res_ref[0] = residual
    upd_ref[0] = own - residual / denominator


def store(res_ref, upd_ref, res_hbm, upd_hbm, sem):
    copies = [
        pltpu.make_async_copy(src, dst, sem.at[k])
        for k, (src, dst) in enumerate(((res_ref, res_hbm), (upd_ref, upd_hbm)))
    ]
    for copy in copies:
        copy.start()
    for copy in copies:
        copy.wait()


def shards(amplitudes, ranks, neighbours, intersections, couplings, energies, factors):
    pairs = lax.axis_size("pair")
    width = amplitudes.shape[1]
    half_w = width // 2
    slots = neighbours.shape[1]
    span = factors.shape[2]
    out = jax.ShapeDtypeStruct((1, half_w, width), jnp.float32)
    hbm = pl.BlockSpec(memory_space=pltpu.HBM)
    vmem = pl.BlockSpec(memory_space=pltpu.VMEM)
    dma = pltpu.SemaphoreType.DMA
    tiles = (2 * REACH + 1, RING)
    operands = [
        operand if operand.ndim == 1 else pltpu.with_memory_space_constraint(operand, pltpu.HBM)
        for operand in (amplitudes, ranks, neighbours, intersections, couplings, energies, factors)
    ]
    results = pl.pallas_call(
        functools.partial(body, pairs),
        out_shape=(out, out),
        in_specs=[hbm, pl.BlockSpec(memory_space=pltpu.SMEM)] + [hbm] * 5,
        out_specs=(vmem, vmem),
        scratch_shapes=[
            pltpu.VMEM(tiles + (width, half_w), jnp.bfloat16),
            pltpu.VMEM((2 * slots, width, width), jnp.bfloat16),
            pltpu.VMEM((2, span, width), jnp.bfloat16),
            pltpu.VMEM((width, width), jnp.float32),
            pltpu.VMEM((half_w, width), jnp.float32),
            pltpu.VMEM((half_w, width), jnp.float32),
            pltpu.VMEM((half_w, width), jnp.bfloat16),
            pltpu.VMEM((1, width), jnp.float32),
            pltpu.SMEM((2, slots), jnp.int32),
            pltpu.SMEM((2, slots), jnp.float32),
            dma((7,)),
            dma((3,)),
            dma((3,)),
            dma((13 + 3 * (2 * REACH + 1),)),
            dma(tiles + (PIECES,)),
            dma((2,)),
            pltpu.SemaphoreType.REGULAR((2,)),
        ],
        compiler_params=pltpu.CompilerParams(
            collective_id=0, has_side_effects=True, vmem_limit_bytes=VMEM_LIMIT
        ),
    )(*operands)
    return pl.pallas_call(
        store,
        out_shape=(out, out),
        in_specs=[vmem, vmem],
        out_specs=(hbm, hbm),
        scratch_shapes=[dma((2,))],
        compiler_params=pltpu.CompilerParams(vmem_limit_bytes=1 << 20),
    )(*results)


VMEM_LIMIT = 12000000


def solution(mesh):
    return jax.shard_map(
        shards,
        mesh=mesh,
        in_specs=(
            P("pair", None, None),
            P("pair"),
            P("pair", "aux"),
            P("pair", "aux", None, None),
            P("pair", "aux"),
            P("pair", None),
            P("pair", None, "aux", None),
        ),
        out_specs=(P("pair", "aux", None), P("pair", "aux", None)),
        check_vma=False,
    )
```

```python
import functools

import jax
import jax.numpy as jnp
from jax import lax
from jax.experimental import pallas as pl
from jax.experimental.pallas import tpu as pltpu
from jax.sharding import PartitionSpec as P

WIN = 8
RING = 4
REACH = WIN // RING
PIECES = 2
MESH = pl.DeviceIdType.MESH


def body(
    pairs,
    amp_hbm,
    ranks_smem,
    nbr_hbm,
    inter_hbm,
    coup_hbm,
    energy_hbm,
    fact_hbm,
    res_ref,
    upd_ref,
    tbuf,
    sbuf,
    fbuf,
    acc,
    send_half,
    recv_half,
    own_rows,
    energy,
    nbr_s,
    coup_s,
    loc_sem,
    s_send,
    s_recv,
    t_send,
    t_recv,
    r_sem,
    hello,
):
    width = amp_hbm.shape[1]
    half_w = width // 2
    slots = nbr_hbm.shape[1]
    rows_all = pairs // RING
    p = lax.axis_index("pair")
    c = lax.axis_index("aux")
    other = 1 - c
    sibling = (p, other)
    x = lax.rem(p, RING)
    row = p // RING
    cols = pl.ds(pl.multiple_of(c * half_w, half_w), half_w)

    def column(dx):
        return lax.rem(x + dx + RING, RING)

    def far_row(dy):
        return lax.rem(row + dy + rows_all, rows_all)

    def chip(dx, dy):
        return (far_row(dy) * RING + column(dx), c)

    def local(src, dst, k):
        return pltpu.make_async_copy(src, dst, loc_sem.at[k])

    own_tile = tbuf.at[REACH, x]
    loads = [
        local(amp_hbm.at[0, :, cols], own_tile, 1),
        local(energy_hbm, energy, 0),
        local(nbr_hbm.at[0], nbr_s.at[c], 2),
        local(coup_hbm.at[0], coup_s.at[c], 3),
        local(fact_hbm.at[0], fbuf, 4),
        local(inter_hbm.at[0], sbuf.at[pl.ds(c * slots, slots)], 5),
        local(amp_hbm.at[0, cols, :], own_rows, 6),
    ]
    loads[0].start()

    barrier = pltpu.get_barrier_semaphore()
    even = lax.rem(row, 2) == 0

    def greet(sem, peer):
        pl.semaphore_signal(sem, inc=1, device_id=peer, device_id_type=MESH)

    pl.when(even)(lambda: greet(barrier, chip(0, -2)))
    callers = [chip(dx, 0) for dx in (2, 1, 3)] + [chip(0, -1), sibling]
    for peer in callers:
        greet(barrier, peer)
    for copy in loads[1:]:
        copy.start()

    loads[0].wait()
    rank = ranks_smem[0]
    row_id = lax.broadcasted_iota(jnp.int32, (width, half_w), 0)
    col_id = lax.broadcasted_iota(jnp.int32, (width, half_w), 1) + c * half_w
    own_tile[...] = jnp.where(
        (row_id < rank) & (col_id < rank), own_tile[...].astype(jnp.float32), 0.0
    ).astype(jnp.bfloat16)

    pl.semaphore_wait(barrier, len(callers) + jnp.where(even, 1, 0))

    def piece(r, xs, h):
        return tbuf.at[r, xs, pl.ds(h * (width // PIECES), width // PIECES)]

    def send(r, xs, home, k, peer):
        def copy(src, dst, recv_sem):
            return pltpu.make_async_remote_copy(
                src_ref=src, dst_ref=dst, send_sem=t_send.at[k], recv_sem=recv_sem,
                device_id=peer, device_id_type=MESH,
            )

        parts = [
            copy(piece(r, xs, h), piece(home, xs, h), t_recv.at[home, xs, h]) for h in range(PIECES)
        ]
        return parts, copy(tbuf.at[r, xs], tbuf.at[home, xs], t_recv.at[home, xs, 0])

    def start(copies):
        for copy in copies[0]:
            copy.start()

    def sent(group):
        for _, whole in group:
            whole.wait_send()

    top = rows_all - 1
    across = column(2)
    up = [send(REACH, x, REACH - dy, dy - 1, chip(0, dy)) for dy in (1, 2)]
    down = [send(REACH, x, REACH + dy, 1 + dy, chip(0, -dy)) for dy in (1, 2)]
    side = [send(REACH, x, REACH, 3 + dx, chip(dx, 0)) for dx in (2, 1, 3)]
    pass_up = send(REACH, across, REACH - 1, 7, chip(0, 1))
    pass_down = send(REACH, across, REACH + 1, 8, chip(0, -1))
    hand_up = send(REACH - 1, x, REACH - 2, 9, chip(0, 1))
    hand_down = send(REACH + 1, x, REACH + 2, 10, chip(0, -1))
    hand_two = send(REACH - 1, across, 0, 23, chip(0, 1))
    hands_two = (row == 0) & (across > x)
    always = up[:1] + side + down[:1] + [pass_up, pass_down]
    if_even = [up[1], down[1], hand_up, hand_down]
    pl.when(even)(lambda: start(up[1]))
    start(up[0])
    greet(hello.at[0], chip(0, 1))
    pl.when(even)(lambda: greet(hello.at[1], chip(0, 2)))
    for copies in side:
        start(copies)

    def send_down(dy):
        def act():
            pl.semaphore_wait(hello.at[dy - 1], 1)
            start(down[dy - 1])

        if dy == 2:
            pl.when(even)(act)
        else:
            act()

    shares = []
    for k, (src, dst) in enumerate(
        (
            (nbr_hbm.at[0], nbr_s.at[c]),
            (coup_hbm.at[0], coup_s.at[c]),
            (inter_hbm.at[0], sbuf.at[pl.ds(c * slots, slots)]),
        )
    ):
        shares.append(
            pltpu.make_async_remote_copy(
                src_ref=src, dst_ref=dst, send_sem=s_send.at[k], recv_sem=s_recv.at[k],
                device_id=sibling, device_id_type=MESH,
            )
        )
    for copy in shares:
        copy.start()

    for copy in loads[1:]:
        copy.wait()
    acc[...] = lax.dot_general(
        fbuf[0], fbuf[1], (((0,), (0,)), ((), ())), preferred_element_type=jnp.float32
    )

    side_of = jnp.where(row < REACH, 1, -1)

    def late(dy):
        low = (row < dy) & ((row > 0) | (c == 1))
        return low | (top - row < dy)

    def soon(dy):
        return jnp.logical_not(late(dy))

    for dy in (1, 2):
        pl.when(jnp.logical_not(row < dy))(functools.partial(send_down, dy))
    def arrived(r, xs, pieces=range(PIECES)):
        for h in pieces:
            part = piece(r, xs, h)
            pltpu.make_async_copy(part, part, t_recv.at[r, xs, h]).wait()

    def wanted(r, source, dest):
        return ((r > 0) | (dest <= source)) & ((r < 2 * REACH) | (dest >= source))

    def relay_copies(r):
        outer = ((r == 0) & (row != 1)) | (r == 2 * REACH)
        copies = []
        for k, dx in enumerate((2, 1, 3)):
            needed = wanted(r, x, column(dx))
            if dx == 2:
                needed &= outer
            copies.append((needed, send(r, x, r, 11 + 3 * (r - jnp.where(r > REACH, 1, 0)) + k, chip(dx, 0))))
        return copies

    def relay(r):
        copies = relay_copies(r)
        for h in range(PIECES):
            arrived(r, x, (h,))
            pl.when(even & (r == REACH - 1))(hand_up[0][h].start)
            pl.when(even & (r == REACH + 1) & (row > 0))(hand_down[0][h].start)
            for needed, parts in copies:
                pl.when(needed)(parts[0][h].start)

    def entry_of(r, xs):
        q = far_row(r - REACH) * RING + xs
        core, at = jnp.int32(0), jnp.int32(0)
        for k in range(2):
            for n in range(slots):
                hit = nbr_s[k, n] == q
                core, at = jnp.where(hit, k, core), jnp.where(hit, n, at)
        return core * slots + at, jnp.where(nbr_s[core, at] == q, coup_s[core, at], 0.0)

    def picks_of(r):
        found = []
        for dx in (0, 1, 3, 2):
            xs = column(dx)
            needed = wanted(r, xs, x)
            slot, factor = entry_of(r, xs)
            found.append((jnp.where(needed, xs, x), slot, jnp.where(needed, factor, 0.0)))
        for dx in (1, 3, 2):
            xs = column(dx)
            due = wanted(r, xs, x)
            if dx == 2:
                due &= (r != REACH) & ((r != REACH - 1) | (row > 0))
            pl.when(due)(functools.partial(arrived, r, xs))
        return found

    def add_products(r, picks, span):
        total = acc[span, :]
        for xs, slot, factor in picks:
            half = jnp.dot(
                sbuf[slot, span, :], tbuf[r, xs], preferred_element_type=jnp.float32
            ).astype(jnp.bfloat16)
            total += factor * lax.dot_general(
                half, sbuf[slot, :, cols], (((1,), (1,)), ((), ())), preferred_element_type=jnp.float32
            )
        return total

    def couple_row(r):
        acc[...] = add_products(r, picks_of(r), pl.ds(0, width))

    for h in range(PIECES):
        arrived(REACH, across, (h,))
        pass_up[0][h].start()
        pl.when(row > 0)(pass_down[0][h].start)
    for dy in (1, 2):
        relay(REACH + dy * side_of)

    def other_side(dy):
        def release():
            send_down(dy)
            if dy == 1:
                start(pass_down)
                start(hand_down)

        pl.when(row < dy)(release)
        relay(REACH - dy * side_of)

    for dy in (1, 2):
        pl.when(soon(dy))(functools.partial(other_side, dy))

    for copy in shares:
        copy.wait()

    def hand_across():
        for h in range(PIECES):
            arrived(REACH - 1, across, (h,))
            pl.when(hands_two)(hand_two[0][h].start)

    @pl.loop(0, REACH + 1)
    def _(k):
        couple_row(REACH + k * side_of)
        pl.when((row == 0) & (c == 0) & (k == 1))(hand_across)

    for dy in (1, 2):
        pl.when(late(dy))(functools.partial(other_side, dy))

    pl.when((row == 0) & (c == 1))(hand_across)

    @pl.loop(1, REACH)
    def _(k):
        couple_row(REACH - k * side_of)

    theirs = pl.ds(pl.multiple_of(other * half_w, half_w), half_w)
    last = REACH - REACH * side_of
    picks = picks_of(last)
    send_half[...] = add_products(last, picks, theirs)
    ship = pltpu.make_async_remote_copy(
        src_ref=send_half, dst_ref=recv_half, send_sem=r_sem.at[0], recv_sem=r_sem.at[1],
        device_id=sibling, device_id_type=MESH,
    )
    ship.start()
    mine = add_products(last, picks, cols)
    rows = lax.broadcasted_iota(jnp.int32, (half_w, width), 0) + c * half_w
    columns = lax.broadcasted_iota(jnp.int32, (half_w, width), 1)
    live = (rows < rank) & (columns < rank)
    by_row = jnp.transpose(jnp.broadcast_to(energy[:, cols], (half_w, half_w)))
    denominator = jnp.concatenate([by_row, by_row], axis=1) + energy[...]
    own = jnp.where(live, own_rows[...].astype(jnp.float32), 0.0)
    sent(always)
    pl.when(even)(lambda: sent(if_even))
    pl.when(hands_two)(lambda: sent([hand_two]))

    @pl.loop(0, 2 * REACH + 1)
    def _(r):
        for needed, copies in relay_copies(r):
            pl.when(needed & (r != REACH))(functools.partial(sent, [copies]))

    here = mine + denominator * own
    ship.wait()
    residual = jnp.where(live, here + recv_half[...], 0.0)
    res_ref[0] = residual
    upd_ref[0] = own - residual / denominator


def store(res_ref, upd_ref, res_hbm, upd_hbm, sem):
    copies = [
        pltpu.make_async_copy(src, dst, sem.at[k])
        for k, (src, dst) in enumerate(((res_ref, res_hbm), (upd_ref, upd_hbm)))
    ]
    for copy in copies:
        copy.start()
    for copy in copies:
        copy.wait()


def shards(amplitudes, ranks, neighbours, intersections, couplings, energies, factors):
    pairs = lax.axis_size("pair")
    width = amplitudes.shape[1]
    half_w = width // 2
    slots = neighbours.shape[1]
    span = factors.shape[2]
    out = jax.ShapeDtypeStruct((1, half_w, width), jnp.float32)
    hbm = pl.BlockSpec(memory_space=pltpu.HBM)
    vmem = pl.BlockSpec(memory_space=pltpu.VMEM)
    dma = pltpu.SemaphoreType.DMA
    tiles = (2 * REACH + 1, RING)
    operands = [
        operand if operand.ndim == 1 else pltpu.with_memory_space_constraint(operand, pltpu.HBM)
        for operand in (amplitudes, ranks, neighbours, intersections, couplings, energies, factors)
    ]
    results = pl.pallas_call(
        functools.partial(body, pairs),
        out_shape=(out, out),
        in_specs=[hbm, pl.BlockSpec(memory_space=pltpu.SMEM)] + [hbm] * 5,
        out_specs=(vmem, vmem),
        scratch_shapes=[
            pltpu.VMEM(tiles + (width, half_w), jnp.bfloat16),
            pltpu.VMEM((2 * slots, width, width), jnp.bfloat16),
            pltpu.VMEM((2, span, width), jnp.bfloat16),
            pltpu.VMEM((width, width), jnp.float32),
            pltpu.VMEM((half_w, width), jnp.float32),
            pltpu.VMEM((half_w, width), jnp.float32),
            pltpu.VMEM((half_w, width), jnp.bfloat16),
            pltpu.VMEM((1, width), jnp.float32),
            pltpu.SMEM((2, slots), jnp.int32),
            pltpu.SMEM((2, slots), jnp.float32),
            dma((7,)),
            dma((3,)),
            dma((3,)),
            dma((12 + 3 * 2 * REACH,)),
            dma(tiles + (PIECES,)),
            dma((2,)),
            pltpu.SemaphoreType.REGULAR((2,)),
        ],
        compiler_params=pltpu.CompilerParams(
            collective_id=0, has_side_effects=True, vmem_limit_bytes=VMEM_LIMIT
        ),
    )(*operands)
    return pl.pallas_call(
        store,
        out_shape=(out, out),
        in_specs=[vmem, vmem],
        out_specs=(hbm, hbm),
        scratch_shapes=[dma((2,))],
        compiler_params=pltpu.CompilerParams(vmem_limit_bytes=1 << 20),
    )(*results)


VMEM_LIMIT = 12000000


def solution(mesh):
    return jax.shard_map(
        shards,
        mesh=mesh,
        in_specs=(
            P("pair", None, None),
            P("pair"),
            P("pair", "aux"),
            P("pair", "aux", None, None),
            P("pair", "aux"),
            P("pair", None),
            P("pair", None, "aux", None),
        ),
        out_specs=(P("pair", "aux", None), P("pair", "aux", None)),
        check_vma=False,
    )
```
